256 devices in a mesh: row: 32 (over y, x, core), col: 8 (over z).
Axes of the slice: x: 4, y: 4, z: 8, core: 2. Of those that a mesh axis runs over, the one named last changes fastest.
Arguments:
- values: float32 [4, 32, 128, 16, 8, 128], P(None, 'row', None, None, 'col'), may hold values from -6 to 6
- fill: int32 [4, 32, 16, 8], P(None, 'row', None, 'col'), may hold values 0 or 1
- inverses: float32 [2, 128, 128], replicated, may hold values from -0.06 to 0.26
- pivots: int32 [2, 128], replicated, may hold values from 0 to 127, each once within a row
Outputs:
- factored: float32 [4, 32, 128, 16, 8, 128], P(None, 'row', None, None, 'col')
The draws below stay inside these ranges and needn't reach their ends.
Inputs may be any that keep to these rules, and one draw needn't show every extreme that they name: `pivots`: each row lists 0 to 127 once.
All inputs are finite; a program needn't handle non-finite values. No bound on the sum of `fill` on one device may be relied on, other than what follows from the above.
Results may differ from the reference program's by a relative error of at most 0.0001.
Values sent between devices are 32-bit elements; how exact they have to be, the bound alone decides.
A program may use at most 128 MiB of HBM per device.

```python
import math
import jax
import jax.numpy as jnp
from jax import lax

B = 128
RB = 4
CB = 16
N_ROW = 32
N_COL = 8


def draw_inverses(key, part):
    key_diag, key_off = jax.random.split(jax.random.fold_in(key, 17))
    diag_vals = jnp.exp(jax.random.uniform(key_diag, (2, B), jnp.float32, math.log(0.05), math.log(0.2)))
    off_vals = jnp.clip(0.012 * jax.random.normal(key_off, (2, B, B), jnp.float32), -0.05, 0.05)
    return off_vals + jnp.eye(B, dtype=jnp.float32)[None] * diag_vals[:, :, None]


def place_ends(entries, rng, least, high):
    extent = entries.shape
    index_at = [jax.random.randint(jax.random.fold_in(rng, axis), (), 0, extent[axis]) for axis in range(len(extent))]
    entries = entries.at[tuple(index_at)].set(least)
    longest = extent.index(max(extent))
    index_at[longest] = (index_at[longest] + 1) % extent[longest]
    return entries.at[tuple(index_at)].set(high)


def block_scale(rng, shape, cuts, least, top_value):
    factor_of, own = 1.0, jax.random.fold_in(rng, 6)
    for position, shards_of in cuts:
        steps = jnp.exp(jax.random.uniform(jax.random.fold_in(own, position), (shards_of,), jnp.float32, least / len(cuts), top_value / len(cuts)))
        factor_of = factor_of * jnp.repeat(steps, shape[position] // shards_of).reshape([-1 if axis == position else 1 for axis in range(len(shape))])
    return factor_of


def bell_draw(own_key, dims, deviation, limit, cuts=(), kind=jnp.bfloat16):
    level = block_scale(own_key, dims, cuts, -0.22, 0.18) if cuts else 1.0
    result = jax.random.normal(own_key, dims, jnp.float32) * deviation * level
    return jnp.minimum(jnp.maximum(result, -limit), limit).astype(kind)


def setup_inputs(seed: int = 0) -> dict:
    keys = jax.random.split(jax.random.key(seed), 5)
    values = bell_draw(keys[0], (RB, N_ROW, B, CB, N_COL, B), 1.0, 6.0, ((1, 32), (4, 8)), jnp.float32)
    fill = place_ends((jax.random.randint(keys[1], (RB, N_ROW, CB, N_COL), 0, 5) < 3).astype(jnp.int32), jax.random.fold_in(keys[1], 1), 0, 1)
    inverses = draw_inverses(jax.random.fold_in(keys[4], 71), 0)
    pivots = jax.vmap(lambda own: jax.random.permutation(own, B))(jax.random.split(keys[3], 2)).reshape((2, B)).astype(jnp.int32)
    return {"values": values, "fill": fill, "inverses": inverses, "pivots": pivots}


def reference(values, fill, inverses, pivots):
    block_rows = RB * N_ROW
    block_cols = CB * N_COL
    size_b = values.shape[2]
    fill_mask = fill.reshape(block_rows, block_cols).astype(values.dtype)
    matrix = values.reshape(block_rows, size_b, block_cols, size_b) * fill_mask[:, None, :, None]
    row_index = jnp.arange(block_rows)
    col_index = jnp.arange(block_cols)
    for step in range(2):
        row_blocks = matrix[step]
        permuted = jnp.take(row_blocks, pivots[step], axis=0)
        u_row = jnp.where((col_index >= step)[None, :, None], permuted, row_blocks)
        matrix = matrix.at[step].set(u_row)
        col_blocks = matrix[:, :, step, :]
        below = (row_index > step)[:, None, None]
        factored = jnp.einsum("ipm,mq->ipq", col_blocks, inverses[step], precision=lax.Precision.HIGHEST)
        l_col = jnp.where(below, factored, col_blocks)
        matrix = matrix.at[:, :, step, :].set(l_col)
        l_panel = jnp.where(below, l_col, 0.0)
        u_panel = jnp.where((col_index > step)[None, :, None], u_row, 0.0)
        update = jnp.einsum("ipm,mjq->ipjq", l_panel, u_panel, precision=lax.Precision.HIGHEST)
        matrix = matrix - fill_mask[:, None, :, None] * update
    return matrix.reshape(values.shape)
```

```python
import jax
import jax.numpy as jnp
from jax import lax
from jax.experimental import pallas as pl
from jax.experimental.pallas import tpu as pltpu
from jax.sharding import PartitionSpec as P

HIGH = lax.Precision.HIGHEST
F32 = jnp.float32
BF16 = jnp.bfloat16
B = 128
RB = 4
CB = 16
NX = 4
NY = 4
NZ = 8
PANEL = CB * B + 256
TREE = PANEL // 4
LBLK = B + 16
LHALF = 2 * LBLK
N = 9
NL = 9
LAG = 2
R = TREE // N
RL = LHALF // NL


def split(x):
    hi = x.astype(BF16)
    return hi, (x - hi.astype(F32)).astype(BF16)


def dot3(a, b):
    mm = lambda u, v: jnp.dot(u, v, preferred_element_type=F32)
    return mm(a[0], b[0]) + (mm(a[0], b[1]) + mm(a[1], b[0]))


def high(a, b, dims=((1,), (0,))):
    return lax.dot_general(a, b, (dims, ((), ())), precision=HIGH, preferred_element_type=F32)


def kernel(values, fill, inverses, pivots, out, vals, u, lp, gmat, pmat, left, load_sem, out_sem,
           urecv, usib, usend, lrecv, lsend, esend, erecv):
    row = lax.axis_index("row")
    z = lax.axis_index("col")
    core = row % 2
    x = (row // 2) % NX
    y = row // (2 * NX)
    other = 1 - core
    e_src = 1 - core

    def at(x_, y_, core_, z_):
        return {"row": (y_ * NX + x_) * 2 + core_, "col": z_}

    xp, xm = (x + 1) % NX, (x + NX - 1) % NX
    yp, ym = (y + 1) % NY, (y + NY - 1) % NY
    zp, zm = (z + 1) % NZ, (z + NZ - 1) % NZ
    sibling = at(x, y, other, z)
    near = [at(xp, y, core, z), at(xm, y, core, z), at(x, yp, core, z), at(x, ym, core, z),
            at(x, y, core, zp), at(x, y, core, zm), sibling]
    is_root = row < 2

    def load(r, c):
        return pltpu.make_async_copy(values.at[r, :, c, 0, :], vals.at[r, c], load_sem.at[r, c])

    @pl.loop(0, CB)
    def _(c):
        load(0, c).start()

    for r in range(1, RB):
        load(r, 0).start()

    barrier = pltpu.get_barrier_semaphore()
    for dev in near:
        pl.semaphore_signal(barrier, inc=1, device_id=dev)

    @pl.when(is_root & (z == e_src))
    def _():
        @pl.loop(1, NZ)
        def _(j):
            pl.semaphore_signal(barrier, inc=1, device_id=at(x, y, core, (z + j) % NZ))

    @pl.when(is_root & (z != e_src))
    def _():
        pl.semaphore_signal(barrier, inc=1, device_id=at(x, y, core, e_src))

    @pl.loop(1, CB)
    def _(c):
        for r in range(1, RB):
            load(r, c).start()

    for k in range(2):
        pt = (lax.broadcasted_iota(jnp.int32, (B, B), 0) == pivots[k:k + 1, :]).astype(F32)
        pmat[k] = pt
        gmat[k] = high(inverses[k], pt, ((1,), (1,)))

    @pl.loop(0, CB)
    def _(c):
        load(0, c).wait()

    for r in range(1, RB):
        load(r, 0).wait()

    @pl.when(is_root)
    def _():
        @pl.loop(0, CB)
        def _(c):
            f = fill[0, 0, c].astype(F32)
            u[core, pl.ds(c * B, B), :] = vals[0, c] * f
            u[core, pl.ds(CB * B + B + c * 8, 8), :] = jnp.zeros((8, B), F32) + f

    @pl.when(z < 2)
    def _():
        for r in range(RB):
            f = fill[r, 0, 0].astype(F32)
            lp[z, pl.ds(r * LBLK, B), :] = vals[r, 0] * f
            lp[z, pl.ds(r * LBLK + B, 16), :] = jnp.zeros((16, B), F32) + f

    pl.semaphore_wait(barrier, len(near) + jnp.where(is_root, jnp.where(z == e_src, NZ - 1, 1), 0))

    def extra(z_):
        return pltpu.make_async_remote_copy(
            src_ref=u.at[core, pl.ds(0, B)], dst_ref=u.at[core, pl.ds(CB * B, B)],
            send_sem=esend.at[z_], recv_sem=erecv, device_id=at(x, y, core, z_))

    @pl.when(is_root & (z == e_src))
    def _():
        @pl.loop(1, NZ)
        def _(j):
            extra((z + j) % NZ).start()

        u[core, pl.ds(CB * B, B), :] = u[core, pl.ds(0, B), :]

    def tree(a, b):
        hops = jnp.where(b == 0, a, jnp.where(a == 0, 4 + b, a + b))
        to_a = ((b == 0) & (a < 3)) | ((b > 0) & (a == 3))
        to_b = (a > 0) & (b < 3)
        return hops, to_a, to_b

    mx, my = (NX - x) % NX, (NY - y) % NY
    trees = []
    for a, b, dev_a, dev_b in ((x, y, near[0], near[2]), (mx, my, near[1], near[3]),
                               (y, x, near[2], near[0]), (my, mx, near[3], near[1])):
        trees.append((*tree(a, b), dev_a, dev_b))
    ways = [[((z - k + NZ) % NZ, near[4]), ((k - z + NZ) % NZ, near[5])] for k in range(2)]

    def chunk(d, i, kind, dev):
        rows = u.at[core, pl.ds(d * TREE + i * R, R)]
        recv = usib.at[d] if kind == 2 else urecv.at[d, i]
        return pltpu.make_async_remote_copy(
            src_ref=rows, dst_ref=rows, send_sem=usend.at[d, kind], recv_sem=recv, device_id=dev)

    def lchunk(k, s, i, dev):
        rows = lp.at[k, pl.ds(s * LHALF + i * RL, RL)]
        return pltpu.make_async_remote_copy(
            src_ref=rows, dst_ref=rows, send_sem=lsend.at[k, s], recv_sem=lrecv.at[k, s, i], device_id=dev)

    @pl.loop(0, LAG * 7 + max(N, NL))
    def _(t):
        for d, (hops, to_a, to_b, dev_a, dev_b) in enumerate(trees):
            i = t - LAG * hops

            @pl.when((i >= 0) & (i < N))
            def _():
                @pl.when(hops > 0)
                def _():
                    chunk(d, i, 0, dev_a).wait_recv()

                if d == 3:
                    @pl.when(is_root & (z != e_src) & (i == (CB * B - 3 * TREE) // R))
                    def _():
                        extra(z).wait_recv()

                @pl.when(to_a)
                def _():
                    chunk(d, i, 0, dev_a).start()

                @pl.when(to_b)
                def _():
                    chunk(d, i, 1, dev_b).start()

                chunk(d, i, 2, sibling).start()

        for k in range(2):
            for s in range(2):
                hops, dev = ways[k][s]
                j = t - LAG * hops

                @pl.when((j >= 0) & (j < NL))
                def _():
                    @pl.when(hops > 0)
                    def _():
                        lchunk(k, s, j, dev).wait_recv()

                    @pl.when(hops < NZ - 1)
                    def _():
                        lchunk(k, s, j, dev).start()

    def whole(d, kind, panel):
        rows = u.at[panel, pl.ds(d * TREE, TREE)]
        return pltpu.make_async_remote_copy(
            src_ref=rows, dst_ref=rows, send_sem=usend.at[d, kind], recv_sem=usib.at[d], device_id=sibling)

    for d in range(4):
        whole(d, 2, other).wait_recv()

    panel = lambda k: jnp.concatenate([lp[k, pl.ds(r * LBLK, B), :] for r in range(RB)], axis=0)
    l_first = high(panel(0), gmat[0])
    u_01 = u[0, pl.ds(CB * B, B), :]
    f_col = jnp.concatenate(
        [jnp.broadcast_to(lp[1, pl.ds(r * LBLK + B, 1), :], (B, B)) for r in range(RB)], axis=0)
    second = panel(1) - f_col * high(l_first, u_01)
    l_second = high(second, gmat[1])
    q10 = split(high(u[1, pl.ds(CB * B, B), :], gmat[0]))
    left[:, 0:B] = l_first
    left[:, B:2 * B] = l_second

    @pl.loop(1, CB)
    def _(c):
        for r in range(1, RB):
            load(r, c).wait()

    @pl.when(is_root)
    def _():
        left[pl.ds(0, B), B:2 * B] = jnp.zeros((B, B), F32)
        own = pmat[core].T

        @pl.loop(0, CB)
        def _(c):
            vals[0, c] = high(own, vals[0, c])

    @pl.when(row == 0)
    def _():
        left[pl.ds(0, B), 0:B] = jnp.zeros((B, B), F32)

    @pl.when(row == 1)
    def _():
        left[pl.ds(0, B), 0:B] = high(pmat[1].T, left[pl.ds(0, B), 0:B])

    lhs = split(left[...])

    def store(r, c):
        return pltpu.make_async_copy(vals.at[r, c], out.at[r, :, c, 0, :], out_sem.at[r, c])

    @pl.loop(0, CB // 2)
    def _(j):
        c = 2 * j
        pair = lambda k: jnp.concatenate(
            [u[k, pl.ds(pl.multiple_of(c * B, B), B), :],
             u[k, pl.ds(pl.multiple_of(c * B + B, B), B), :]], axis=1)
        top = pair(0)
        top2 = split(top)
        f_row = jnp.concatenate([u[1, pl.ds(CB * B + B + c * 8, 1), :],
                                 u[1, pl.ds(CB * B + B + c * 8 + 8, 1), :]], axis=1)
        low2 = split(pair(1) - f_row * dot3(q10, top2))
        rhs = tuple(jnp.concatenate([a, b], axis=0) for a, b in zip(top2, low2))
        update = dot3(lhs, rhs)
        for r in range(RB):
            for e in range(2):
                f = fill[r, 0, c + e].astype(F32)
                vals[r, c + e] = (vals[r, c + e] - update[r * B:(r + 1) * B, e * B:(e + 1) * B]) * f

        @pl.when((j == 0) & (z < 2))
        def _():
            keep = jnp.where(z == 0, panel(0), second)
            done = high(keep, jnp.where(z == 0, inverses[0], inverses[1]))
            for r in range(RB):
                if r == 0:
                    @pl.when(row > z)
                    def _():
                        vals[0, 0] = done[0:B]
                else:
                    vals[r, 0] = done[r * B:(r + 1) * B]

        for r in range(RB):
            for e in range(2):
                store(r, c + e).start()

    for d, (hops, to_a, to_b, dev_a, dev_b) in enumerate(trees):
        @pl.when(to_a)
        def _():
            whole(d, 0, core).wait_send()

        @pl.when(to_b)
        def _():
            whole(d, 1, core).wait_send()

        whole(d, 2, core).wait_send()

    for k in range(2):
        for s in range(2):
            hops, dev = ways[k][s]

            @pl.when(hops < NZ - 1)
            def _():
                rows = lp.at[k, pl.ds(s * LHALF, LHALF)]
                pltpu.make_async_remote_copy(
                    src_ref=rows, dst_ref=rows, send_sem=lsend.at[k, s], recv_sem=lrecv.at[k, s, 0],
                    device_id=dev).wait_send()

    @pl.when(is_root & (z == e_src))
    def _():
        @pl.loop(1, NZ)
        def _(j):
            extra((z + j) % NZ).wait_send()

    @pl.loop(0, CB)
    def _(c):
        for r in range(RB):
            store(r, c).wait()


def per_device(values, fill, inverses, pivots):
    shape = (RB, B, CB, 1, B)
    vmem = pl.BlockSpec(memory_space=pltpu.VMEM)
    result = pl.pallas_call(
        kernel,
        out_shape=jax.ShapeDtypeStruct(shape, F32),
        in_specs=[pl.BlockSpec(memory_space=pltpu.HBM), pl.BlockSpec(memory_space=pltpu.SMEM), vmem, vmem],
        out_specs=pl.BlockSpec(memory_space=pl.ANY),
        scratch_shapes=[
            pltpu.VMEM((RB, CB, B, B), F32),
            pltpu.VMEM((2, PANEL, B), F32),
            pltpu.VMEM((2, RB * LBLK, B), F32),
            pltpu.VMEM((2, B, B), F32),
            pltpu.VMEM((2, B, B), F32),
            pltpu.VMEM((RB * B, 2 * B), F32),
            pltpu.SemaphoreType.DMA((RB, CB)),
            pltpu.SemaphoreType.DMA((RB, CB)),
            pltpu.SemaphoreType.DMA((4, N)),
            pltpu.SemaphoreType.DMA((4,)),
            pltpu.SemaphoreType.DMA((4, 3)),
            pltpu.SemaphoreType.DMA((2, 2, NL)),
            pltpu.SemaphoreType.DMA((2, 2)),
            pltpu.SemaphoreType.DMA((NZ,)),
            pltpu.SemaphoreType.DMA(()),
        ],
        compiler_params=pltpu.CompilerParams(
            collective_id=0, has_side_effects=True, vmem_limit_bytes=24 << 20),
    )(values.reshape(shape), fill.reshape(RB, 1, CB), inverses, pivots)
    return result.reshape(values.shape)


def solution(mesh):
    placed = (P(None, "row", None, None, "col", None), P(None, "row", None, "col"), P(), P())
    return jax.shard_map(
        per_device,
        mesh=mesh,
        in_specs=placed,
        out_specs=P(None, "row", None, None, "col", None),
        check_vma=False,
    )
```

```python
import jax
import jax.numpy as jnp
from jax import lax
from jax.experimental import pallas as pl
from jax.experimental.pallas import tpu as pltpu
from jax.sharding import PartitionSpec as P

HIGH = lax.Precision.HIGHEST
F32 = jnp.float32
BF16 = jnp.bfloat16
B = 128
RB = 4
CB = 16
NX = 4
NY = 4
NZ = 8
EXTRA = CB * B
ER = 40
PANEL = EXTRA + 4 * ER
N = 8
R = CB * B // 4 // N
NL = 8
RL = RB * B // NL
LAG = 7


def split(x):
    hi = x.astype(BF16)
    return hi, (x - hi.astype(F32)).astype(BF16)


def dot3(a, b):
    mm = lambda u, v: jnp.dot(u, v, preferred_element_type=F32)
    return mm(a[0], b[0]) + (mm(a[0], b[1]) + mm(a[1], b[0]))


def high(a, b, dims=((1,), (0,))):
    return lax.dot_general(a, b, (dims, ((), ())), precision=HIGH, preferred_element_type=F32)


def kernel(values, fill_hbm, inverses_hbm, pivots_hbm, out, vals, u, lp, fcol, gmat, pmat, left, fill, inverses,
           pivots, load_sem, out_sem, small_sem, urecv, usib, usend, lrecv, lsend, frecv, fsend, esend, erecv):
    row = lax.axis_index("row")
    z = lax.axis_index("col")
    core = row % 2
    x = (row // 2) % NX
    y = row // (2 * NX)
    other = 1 - core
    e_src = 1 - core

    def at(x_, y_, core_, z_):
        return {"row": (y_ * NX + x_) * 2 + core_, "col": z_}

    zp, zm = (z + 1) % NZ, (z + NZ - 1) % NZ
    sibling = at(x, y, other, z)
    cube = [at(x + 1 - 2 * (x % 2), y, core, z), at(3 - x, y, core, z),
            at(x, y + 1 - 2 * (y % 2), core, z), at(x, 3 - y, core, z)]
    bits = [(x + 1) // 2 % 2, x // 2, (y + 1) // 2 % 2, y // 2]
    near = cube + [at(x, y, core, zp), at(x, y, core, zm), sibling]
    is_root = row < 2

    def load(r, c):
        return pltpu.make_async_copy(values.at[r, :, c, 0, :], vals.at[r, c], load_sem.at[r, c])

    small = [pltpu.make_async_copy(fill_hbm, fill, small_sem.at[0]),
             pltpu.make_async_copy(pivots_hbm, pivots, small_sem.at[1]),
             pltpu.make_async_copy(inverses_hbm, inverses, small_sem.at[2])]
    for copy in small:
        copy.start()

    @pl.loop(0, CB)
    def _(c):
        load(0, c).start()

    for r in range(1, RB):
        load(r, 0).start()

    barrier = pltpu.get_barrier_semaphore()
    for dev in near:
        pl.semaphore_signal(barrier, inc=1, device_id=dev)

    @pl.when(is_root & (z == e_src))
    def _():
        @pl.loop(1, NZ)
        def _(j):
            pl.semaphore_signal(barrier, inc=1, device_id=at(x, y, core, (z + j) % NZ))

    @pl.when(is_root & (z != e_src))
    def _():
        pl.semaphore_signal(barrier, inc=1, device_id=at(x, y, core, e_src))

    @pl.loop(1, CB)
    def _(c):
        for r in range(1, RB):
            load(r, c).start()

    for copy in small:
        copy.wait()

    for k in range(2):
        pt = (lax.broadcasted_iota(jnp.int32, (B, B), 0) == pivots[k:k + 1, :]).astype(F32)
        pmat[k] = pt
        gmat[k] = high(inverses[k], pt, ((1,), (1,)))

    load(0, 0).wait()

    @pl.when(is_root)
    def _():
        u[core, 0:B, :] = vals[0, 0] * fill[0, 0, 0].astype(F32)

    pl.semaphore_wait(barrier, len(near) + jnp.where(is_root, jnp.where(z == e_src, NZ - 1, 1), 0))

    def extra(z_):
        return pltpu.make_async_remote_copy(
            src_ref=u.at[core, pl.ds(0, B)], dst_ref=u.at[core, pl.ds(EXTRA, B)],
            send_sem=esend.at[z_], recv_sem=erecv, device_id=at(x, y, core, z_))

    @pl.when(is_root & (z == e_src))
    def _():
        @pl.loop(1, NZ)
        def _(j):
            extra((z + j) % NZ).start()

        u[core, pl.ds(EXTRA, B), :] = u[core, pl.ds(0, B), :]

    @pl.loop(1, CB)
    def _(c):
        load(0, c).wait()

    for r in range(1, RB):
        load(r, 0).wait()

    @pl.when(is_root)
    def _():
        @pl.loop(0, CB)
        def _(c):
            f = fill[0, 0, c].astype(F32)

            @pl.when(c > 0)
            def _():
                u[core, pl.ds(c * B, B), :] = vals[0, c] * f

            u[core, pl.ds(EXTRA + B + c, 1), :] = jnp.zeros((1, B), F32) + f

        u[core, pl.ds(EXTRA + B + CB, CB), :] = jnp.zeros((CB, B), F32)

    @pl.when(z < 2)
    def _():
        for r in range(RB):
            f = fill[r, 0, 0].astype(F32)
            lp[z, pl.ds(r * B, B), :] = vals[r, 0] * f

            @pl.when(z == 1)
            def _():
                fcol[pl.ds(r, 1), :] = jnp.zeros((1, B), F32) + f

    @pl.when(z == 1)
    def _():
        fcol[pl.ds(RB, RB), :] = jnp.zeros((RB, B), F32)

    weight = bits[0] + bits[1] + bits[2] + bits[3]
    top = weight == 0
    trees = []
    for d in range(4):
        rel = [bits[(d + q) % 4] if q < 4 else 1 - bits[d] for q in range(1, 5)]
        last = jnp.where(rel[3] == 1, 4, jnp.where(rel[2] == 1, 3, jnp.where(rel[1] == 1, 2, rel[0])))
        hops = jnp.where(top, 0, 1 + rel[0] + rel[1] + rel[2] + rel[3])
        kids = [((d + q) % 4, last < q) for q in range(1, 4)]
        kids.append((d, top | ((last >= 1) & (last <= 3))))
        trees.append((hops, kids))

    def chunk(d, i, kind, dev):
        rows = u.at[core, pl.ds((4 * (i // 2) + d) * B + i % 2 * R, R)]
        recv = usib.at[d] if kind == 4 else urecv.at[d, i]
        return pltpu.make_async_remote_copy(
            src_ref=rows, dst_ref=rows, send_sem=usend.at[d, kind], recv_sem=recv, device_id=dev)

    def echunk(d, kind, dev):
        rows = u.at[core, pl.ds(EXTRA + d * ER, ER)]
        recv = usib.at[d] if kind == 4 else urecv.at[d, N]
        return pltpu.make_async_remote_copy(
            src_ref=rows, dst_ref=rows, send_sem=usend.at[d, kind], recv_sem=recv, device_id=dev)

    ways = []
    for k in range(2):
        for s in range(2):
            hops = (z - k + NZ) % NZ if s == 0 else (k - z + NZ) % NZ
            count = lambda h: jnp.where(h <= 3, NL, jnp.where(h == 4, NL // 2, 0))
            ways.append((k, s, hops, count(hops), count(hops + 1), near[4 + s]))

    def lchunk(k, s, j, dev):
        rows = lp.at[k, pl.ds((j + s * (NL // 2)) % NL * RL, RL)]
        return pltpu.make_async_remote_copy(
            src_ref=rows, dst_ref=rows, send_sem=lsend.at[k, s], recv_sem=lrecv.at[k, s, j], device_id=dev)

    def fcopy(s):
        return pltpu.make_async_remote_copy(
            src_ref=fcol, dst_ref=fcol, send_sem=fsend.at[s], recv_sem=frecv, device_id=near[4 + s])

    f_up = (z - 1 + NZ) % NZ
    f_to = [f_up <= 3, (f_up == 0) | ((f_up >= 6))]

    @pl.loop(0, LAG * 5 + N + 1)
    def _(t):
        for k, s, hops, get, give, dev in ways:
            j = t - LAG * hops

            @pl.when((j >= 0) & (j < get))
            def _():
                @pl.when(hops > 0)
                def _():
                    lchunk(k, s, j, dev).wait_recv()

                @pl.when(j < give)
                def _():
                    lchunk(k, s, j, dev).start()

        for d, (hops, kids) in enumerate(trees):
            i = t - LAG * hops

            @pl.when((i >= 0) & (i < N))
            def _():
                @pl.when(hops > 0)
                def _():
                    chunk(d, i, d, sibling).wait_recv()

                for m, (bit, has) in enumerate(kids):
                    @pl.when(has)
                    def _():
                        chunk(d, i, m, cube[bit]).start()

                chunk(d, i, 4, sibling).start()

            @pl.when(i == N)
            def _():
                @pl.when(hops > 0)
                def _():
                    echunk(d, d, sibling).wait_recv()

                if d == 0:
                    @pl.when(is_root & (z != e_src))
                    def _():
                        extra(z).wait_recv()

                for m, (bit, has) in enumerate(kids):
                    @pl.when(has)
                    def _():
                        echunk(d, m, cube[bit]).start()

                echunk(d, 4, sibling).start()

        @pl.when(t == LAG * jnp.where(f_up <= 4, f_up, NZ - f_up))
        def _():
            @pl.when(f_up > 0)
            def _():
                fcopy(0).wait_recv()

            for s in range(2):
                @pl.when(f_to[s])
                def _():
                    fcopy(s).start()

    def whole(d, kind, panel):
        rows = u.at[panel, pl.ds(d * (CB * B // 4), CB * B // 4 + ER)]
        return pltpu.make_async_remote_copy(
            src_ref=rows, dst_ref=rows, send_sem=usend.at[d, kind], recv_sem=usib.at[d], device_id=sibling)

    for d in range(4):
        whole(d, 4, other).wait_recv()

    panel = lambda k: lp[k]
    l_first = high(panel(0), gmat[0])
    u_01 = u[0, pl.ds(EXTRA, B), :]
    f_col = jnp.concatenate(
        [jnp.broadcast_to(fcol[pl.ds(r, 1), :], (B, B)) for r in range(RB)], axis=0)
    second = panel(1) - f_col * high(l_first, u_01)
    l_second = high(second, gmat[1])
    q10 = split(high(u[1, pl.ds(EXTRA, B), :], gmat[0]))
    left[:, 0:B] = l_first
    left[:, B:2 * B] = l_second

    @pl.loop(1, CB)
    def _(c):
        for r in range(1, RB):
            load(r, c).wait()

    @pl.when(is_root)
    def _():
        left[pl.ds(0, B), B:2 * B] = jnp.zeros((B, B), F32)
        own = pmat[core].T

        @pl.loop(0, CB)
        def _(c):
            vals[0, c] = high(own, vals[0, c])

    @pl.when(row == 0)
    def _():
        left[pl.ds(0, B), 0:B] = jnp.zeros((B, B), F32)

    @pl.when(row == 1)
    def _():
        left[pl.ds(0, B), 0:B] = high(pmat[1].T, left[pl.ds(0, B), 0:B])

    lhs = split(left[...])

    def store(r, c):
        return pltpu.make_async_copy(vals.at[r, c], out.at[r, :, c, 0, :], out_sem.at[r, c])

    @pl.loop(0, CB // 2)
    def _(j):
        c = 2 * j
        pair = lambda k: jnp.concatenate(
            [u[k, pl.ds(pl.multiple_of(c * B, B), B), :],
             u[k, pl.ds(pl.multiple_of(c * B + B, B), B), :]], axis=1)
        top = pair(0)
        top2 = split(top)
        f_row = jnp.concatenate([u[1, pl.ds(EXTRA + B + c, 1), :],
                                 u[1, pl.ds(EXTRA + B + c + 1, 1), :]], axis=1)
        low2 = split(pair(1) - f_row * dot3(q10, top2))
        rhs = tuple(jnp.concatenate([a, b], axis=0) for a, b in zip(top2, low2))
        update = dot3(lhs, rhs)
        for r in range(RB):
            for e in range(2):
                f = fill[r, 0, c + e].astype(F32)
                vals[r, c + e] = (vals[r, c + e] - update[r * B:(r + 1) * B, e * B:(e + 1) * B]) * f

        @pl.when((j == 0) & (z < 2))
        def _():
            keep = jnp.where(z == 0, panel(0), second)
            done = high(keep, jnp.where(z == 0, inverses[0], inverses[1]))
            for r in range(RB):
                if r == 0:
                    @pl.when(row > z)
                    def _():
                        vals[0, 0] = done[0:B]
                else:
                    vals[r, 0] = done[r * B:(r + 1) * B]

        for r in range(RB):
            for e in range(2):
                store(r, c + e).start()

    for d, (hops, kids) in enumerate(trees):
        for m, (bit, has) in enumerate(kids):
            @pl.when(has)
            def _():
                whole(d, m, core).wait_send()

        whole(d, 4, core).wait_send()

    for k, s, hops, get, give, dev in ways:
        for amount in (NL // 2, NL):
            @pl.when(give == amount)
            def _():
                rows = lp.at[k, pl.ds(0, amount * RL)]
                pltpu.make_async_remote_copy(
                    src_ref=rows, dst_ref=rows, send_sem=lsend.at[k, s], recv_sem=lrecv.at[k, s, 0],
                    device_id=dev).wait_send()

    for s in range(2):
        @pl.when(f_to[s])
        def _():
            fcopy(s).wait_send()

    @pl.when(is_root & (z == e_src))
    def _():
        @pl.loop(1, NZ)
        def _(j):
            extra((z + j) % NZ).wait_send()

    @pl.loop(0, CB)
    def _(c):
        for r in range(RB):
            store(r, c).wait()


def per_device(values, fill, inverses, pivots):
    shape = (RB, B, CB, 1, B)
    hbm = lambda a: pltpu.with_memory_space_constraint(a, pltpu.HBM)
    result = pl.pallas_call(
        kernel,
        out_shape=jax.ShapeDtypeStruct(shape, F32),
        in_specs=[pl.BlockSpec(memory_space=pltpu.HBM)] * 4,
        out_specs=pl.BlockSpec(memory_space=pl.ANY),
        scratch_shapes=[
            pltpu.VMEM((RB, CB, B, B), F32),
            pltpu.VMEM((2, PANEL, B), F32),
            pltpu.VMEM((2, RB * B, B), F32),
            pltpu.VMEM((2 * RB, B), F32),
            pltpu.VMEM((2, B, B), F32),
            pltpu.VMEM((2, B, B), F32),
            pltpu.VMEM((RB * B, 2 * B), F32),
            pltpu.SMEM((RB, 1, CB), jnp.int32),
            pltpu.VMEM((2, B, B), F32),
            pltpu.VMEM((2, B), jnp.int32),
            pltpu.SemaphoreType.DMA((RB, CB)),
            pltpu.SemaphoreType.DMA((RB, CB)),
            pltpu.SemaphoreType.DMA((3,)),
            pltpu.SemaphoreType.DMA((4, N + 1)),
            pltpu.SemaphoreType.DMA((4,)),
            pltpu.SemaphoreType.DMA((4, 5)),
            pltpu.SemaphoreType.DMA((2, 2, NL)),
            pltpu.SemaphoreType.DMA((2, 2)),
            pltpu.SemaphoreType.DMA(()),
            pltpu.SemaphoreType.DMA((2,)),
            pltpu.SemaphoreType.DMA((NZ,)),
            pltpu.SemaphoreType.DMA(()),
        ],
        compiler_params=pltpu.CompilerParams(
            collective_id=0, has_side_effects=True, vmem_limit_bytes=24 << 20),
    )(hbm(values.reshape(shape)), hbm(fill.reshape(RB, 1, CB)), hbm(inverses), hbm(pivots))
    return result.reshape(values.shape)


def solution(mesh):
    placed = (P(None, "row", None, None, "col", None), P(None, "row", None, "col"), P(), P())
    return jax.shard_map(
        per_device,
        mesh=mesh,
        in_specs=placed,
        out_specs=P(None, "row", None, None, "col", None),
        check_vma=False,
    )
```

```python
import jax
import jax.numpy as jnp
from jax import lax
from jax.experimental import pallas as pl
from jax.experimental.pallas import tpu as pltpu
from jax.sharding import PartitionSpec as P

HIGH = lax.Precision.HIGHEST
F32 = jnp.float32
BF16 = jnp.bfloat16
B = 128
RB = 4
CB = 16
NX = 4
NY = 4
NZ = 8
EXTRA = CB * B
ER = 40
PANEL = EXTRA + 4 * ER
N = 8
R = CB * B // 4 // N
NL = 8
RL = RB * B // NL
LA = 4
LB = 2
LROOT = 8


def split(x):
    hi = x.astype(BF16)
    return hi, (x - hi.astype(F32)).astype(BF16)


def dot3(a, b):
    mm = lambda u, v: jnp.dot(u, v, preferred_element_type=F32)
    return mm(a[0], b[0]) + (mm(a[0], b[1]) + mm(a[1], b[0]))


def high(a, b, dims=((1,), (0,))):
    return lax.dot_general(a, b, (dims, ((), ())), precision=HIGH, preferred_element_type=F32)


def kernel(values, fill_hbm, inverses_hbm, pivots_hbm, out, vals, u, lp, fcol, gmat, pmat, left, fill, inverses,
           pivots, load_sem, out_sem, small_sem, urecv, usib, usend, lrecv, lsend, frecv, fsend, esend, erecv,
           ready, eready):
    row = lax.axis_index("row")
    z = lax.axis_index("col")
    core = row % 2
    x = (row // 2) % NX
    y = row // (2 * NX)
    other = 1 - core
    e_src = 1 - core

    def at(x_, y_, core_, z_):
        return {"row": (y_ * NX + x_) * 2 + core_, "col": z_}

    zp, zm = (z + 1) % NZ, (z + NZ - 1) % NZ
    sibling = at(x, y, other, z)
    cube = [at(x + 1 - 2 * (x % 2), y, core, z), at(3 - x, y, core, z),
            at(x, y + 1 - 2 * (y % 2), core, z), at(x, 3 - y, core, z)]
    bits = [(x + 1) // 2 % 2, x // 2, (y + 1) // 2 % 2, y // 2]
    above, below = at(x, y, core, zp), at(x, y, core, zm)
    near = [above, below]
    is_root = row < 2

    def load(r, c):
        return pltpu.make_async_copy(values.at[r, :, c, 0, :], vals.at[r, c], load_sem.at[r, c])

    up, down = z <= 4, (z <= 1) | (z >= 5)
    from_below, from_above = (z >= 1) & (z <= 5), (z == 0) | (z >= 4)
    barrier = pltpu.get_barrier_semaphore()
    for dev in cube + [sibling]:
        pl.semaphore_signal(barrier, inc=1, device_id=dev)

    @pl.when(up)
    def _():
        pl.semaphore_signal(barrier, inc=1, device_id=above)

    @pl.when(down)
    def _():
        pl.semaphore_signal(barrier, inc=1, device_id=below)

    @pl.when(is_root & (z == e_src))
    def _():
        @pl.loop(1, NZ)
        def _(j):
            pl.semaphore_signal(barrier, inc=1, device_id=at(x, y, core, (z + j) % NZ))

    small = [pltpu.make_async_copy(fill_hbm, fill, small_sem.at[0]),
             pltpu.make_async_copy(pivots_hbm, pivots, small_sem.at[1]),
             pltpu.make_async_copy(inverses_hbm, inverses, small_sem.at[2])]
    small[0].start()

    @pl.loop(0, CB)
    def _(n):
        load(0, n % 4 * 4 + n // 4).start()

    for r in range(1, RB):
        load(r, 0).start()

    for copy in small[1:]:
        copy.start()

    @pl.loop(1, CB)
    def _(c):
        for r in range(1, RB):
            load(r, c).start()

    for copy in small:
        copy.wait()

    def inverse_products():
        for k in range(2):
            pt = (lax.broadcasted_iota(jnp.int32, (B, B), 0) == pivots[k:k + 1, :]).astype(F32)
            pmat[k] = pt
            gmat[k] = high(inverses[k], pt, ((1,), (1,)))

    pl.semaphore_wait(barrier, 5 + jnp.where(from_below, 1, 0) + jnp.where(from_above, 1, 0)
                      + jnp.where(is_root & (z != e_src), 1, 0))

    @pl.when(from_below)
    def _():
        pl.semaphore_signal(ready.at[0], inc=1, device_id=below)

    @pl.when(from_above)
    def _():
        pl.semaphore_signal(ready.at[1], inc=1, device_id=above)

    @pl.when(is_root & (z != e_src))
    def _():
        pl.semaphore_signal(eready.at[z], inc=1, device_id=at(x, y, core, e_src))

    def extra(z_):
        return pltpu.make_async_remote_copy(
            src_ref=u.at[core, pl.ds(0, B)], dst_ref=u.at[core, pl.ds(EXTRA, B)],
            send_sem=esend.at[z_], recv_sem=erecv, device_id=at(x, y, core, z_))

    @pl.when(z < 2)
    def _():
        for r in range(RB):
            f = fill[r, 0, 0].astype(F32)
            load(r, 0).wait()
            lp[z, pl.ds(r * B, B), :] = vals[r, 0] * f

            @pl.when(z == 1)
            def _():
                fcol[pl.ds(r, 1), :] = jnp.zeros((1, B), F32) + f

    @pl.when(z == 1)
    def _():
        fcol[pl.ds(RB, RB), :] = jnp.zeros((RB, B), F32)

    @pl.when(z >= 2)
    def _():
        for r in range(RB):
            load(r, 0).wait()

    @pl.when(row >= 2)
    def _():
        @pl.loop(1, CB)
        def _(c):
            load(0, c).wait()

        inverse_products()

    weight = bits[0] + bits[1] + bits[2] + bits[3]
    top = weight == 0
    trees = []
    for d in range(4):
        rel = [bits[(d + q) % 4] if q < 4 else 1 - bits[d] for q in range(1, 5)]
        last = jnp.where(rel[3] == 1, 4, jnp.where(rel[2] == 1, 3, jnp.where(rel[1] == 1, 2, rel[0])))
        hops = jnp.where(top, 0, 1 + rel[0] + rel[1] + rel[2] + rel[3])
        kids = [((d + q) % 4, last < q) for q in range(1, 4)]
        kids.append((d, top | ((last >= 1) & (last <= 3))))
        trees.append((hops, kids))

    def chunk(d, i, kind, dev):
        rows = u.at[core, pl.ds(d * 4 * B + i * R, R)]
        recv = urecv.at[d, i]
        return pltpu.make_async_remote_copy(
            src_ref=rows, dst_ref=rows, send_sem=usend.at[d, kind], recv_sem=recv, device_id=dev)

    def to_sibling(d, i):
        rows = u.at[core, pl.ds(d * 4 * B + (i - 3) * R, 4 * R)]
        return pltpu.make_async_remote_copy(
            src_ref=rows, dst_ref=rows, send_sem=usend.at[d, 4], recv_sem=usib.at[d], device_id=sibling)

    def echunk(d, kind, dev):
        rows = u.at[core, pl.ds(EXTRA + d * ER, ER)]
        recv = usib.at[d] if kind == 4 else urecv.at[d, N]
        return pltpu.make_async_remote_copy(
            src_ref=rows, dst_ref=rows, send_sem=usend.at[d, kind], recv_sem=recv, device_id=dev)

    ways = []
    for k in range(2):
        for s in range(2):
            hops = (z - k + NZ) % NZ if s == 0 else (k - z + NZ) % NZ
            count = lambda h: jnp.where(h <= 3, NL, jnp.where(h == 4, NL // 2, 0))
            ways.append((k, s, hops, count(hops), count(hops + 1), near[s]))

    def lchunk(k, s, j, dev):
        rows = lp.at[k, pl.ds((j + s * (NL // 2)) % NL * RL, RL)]
        return pltpu.make_async_remote_copy(
            src_ref=rows, dst_ref=rows, send_sem=lsend.at[k, s], recv_sem=lrecv.at[k, s, j], device_id=dev)

    def fcopy(s):
        return pltpu.make_async_remote_copy(
            src_ref=fcol, dst_ref=fcol, send_sem=fsend.at[s], recv_sem=frecv, device_id=near[s])

    f_up = (z - 1 + NZ) % NZ
    f_to = [f_up <= 3, (f_up == 0) | ((f_up >= 6))]

    early = [top | (bits[d] == 1) for d in range(4)]
    first_up, first_down = jnp.where(z >= 1, z - 1, 0), jnp.where(z == 1, 0, (NZ - z) % NZ)
    f_hops = jnp.where(f_up <= 4, f_up, NZ - f_up)

    start = jnp.where(top, LROOT, LB)

    def columns(n):
        base = n - start + LA * weight
        for s, (sends, least) in enumerate(((up, first_up), (down, first_down))):
            @pl.when(sends & (base == LA * least))
            def _():
                pl.semaphore_wait(ready.at[s], 1)

        @pl.when(base == LA * f_hops)
        def _():
            @pl.when(f_up > 0)
            def _():
                fcopy(0).wait_recv()

            for s in range(2):
                @pl.when(f_to[s])
                def _():
                    fcopy(s).start()

        for k, s, hops, get, give, dev in ways:
            j = base - LA * hops

            @pl.when((j >= 0) & (j < get))
            def _():
                @pl.when(hops > 0)
                def _():
                    lchunk(k, s, j, dev).wait_recv()

                @pl.when(j < give)
                def _():
                    lchunk(k, s, j, dev).start()

    def rows_of(d, i):
        @pl.when(weight > 0)
        def _():
            chunk(d, i, d, sibling).wait_recv()

        for m, (bit, has) in enumerate(trees[d][1]):
            @pl.when(has)
            def _():
                chunk(d, i, m, cube[bit]).start()

        @pl.when(i % 4 == 3)
        def _():
            to_sibling(d, i).start()

    def extra_of(d):
        @pl.when(weight > 0)
        def _():
            echunk(d, d, sibling).wait_recv()

        for m, (bit, has) in enumerate(trees[d][1]):
            @pl.when(has)
            def _():
                echunk(d, m, cube[bit]).start()

        echunk(d, 4, sibling).start()

    @pl.when(is_root)
    def _():
        for c in range(CB):
            u[core, EXTRA + B + c:EXTRA + B + c + 1, :] = jnp.zeros((1, B), F32) + fill[0, 0, c].astype(F32)

        u[core, EXTRA + B + CB:EXTRA + B + 2 * CB, :] = jnp.zeros((CB, B), F32)

    @pl.loop(jnp.minimum(start - LA * weight, 0), 0)
    def _(n):
        columns(n)

    @pl.loop(0, N)
    def _(i):
        @pl.when(is_root & (i % 2 == 0))
        def _():
            for d in range(4):
                c = 4 * d + i // 2
                if d == 0:
                    @pl.when(i > 0)
                    def _():
                        load(0, c).wait()
                else:
                    load(0, c).wait()

                u[core, pl.ds(c * B, B), :] = vals[0, c] * fill[0, 0, c].astype(F32)

        for d in range(4):
            @pl.when(early[d])
            def _():
                rows_of(d, i)

        @pl.when(is_root & (z == e_src) & (i == 0))
        def _():
            u[core, pl.ds(EXTRA, B), :] = u[core, pl.ds(0, B), :]

            pl.semaphore_wait(eready.at[1 - e_src], 1)
            extra(1 - e_src).start()

        @pl.when(is_root & (z == e_src) & (i == 3))
        def _():
            @pl.loop(2, NZ)
            def _(j):
                pl.semaphore_wait(eready.at[j], 1)
                extra(j).start()

        columns(i)

    @pl.when(is_root & (z != e_src))
    def _():
        extra(z).wait_recv()

    for d in range(4):
        @pl.when(early[d])
        def _():
            extra_of(d)

    @pl.when(is_root)
    def _():
        inverse_products()
        pmat[core] = pmat[core].T

    @pl.loop(N, jnp.maximum(LA * (4 - weight) + start + NL, N))
    def _(n):
        columns(n)

        @pl.when(is_root & (n < N + CB))
        def _():
            own = pmat[core].astype(BF16)
            v = vals[0, n - N]
            first = v.astype(BF16)
            rest = v - first.astype(F32)
            second_ = rest.astype(BF16)
            third = (rest - second_.astype(F32)).astype(BF16)
            mm = lambda a: jnp.dot(own, a, preferred_element_type=F32)
            vals[0, n - N] = mm(first) + (mm(second_) + mm(third))

    panel = lambda k: lp[k]
    for half in range(2):
        if half == 1:
            g_first, g_second = split(gmat[0]), split(gmat[1])
            l_first = dot3(split(panel(0)), g_first)
            left[:, 0:B] = l_first

        for d in range(4):
            @pl.when(~early[d])
            def _():
                @pl.loop(4 * half, 4 * half + 4)
                def _(i):
                    chunk(d, i, d, sibling).wait_recv()

                to_sibling(d, 4 * half + 3).start()

    for d in range(4):
        @pl.when(~early[d])
        def _():
            echunk(d, d, sibling).wait_recv()
            echunk(d, 4, sibling).start()

    def whole(d, kind, panel):
        rows = u.at[panel, pl.ds(d * (CB * B // 4), CB * B // 4 + ER)]
        return pltpu.make_async_remote_copy(
            src_ref=rows, dst_ref=rows, send_sem=usend.at[d, kind], recv_sem=usib.at[d], device_id=sibling)

    @pl.loop(1, CB)
    def _(c):
        for r in range(1, RB):
            load(r, c).wait()

    for d in range(4):
        whole(d, 4, other).wait_recv()

    u_01 = u[0, pl.ds(EXTRA, B), :]
    f_col = jnp.concatenate(
        [jnp.broadcast_to(fcol[pl.ds(r, 1), :], (B, B)) for r in range(RB)], axis=0)
    second = panel(1) - f_col * dot3(split(l_first), split(u_01))
    left[:, B:2 * B] = dot3(split(second), g_second)
    q10 = split(dot3(split(u[1, pl.ds(EXTRA, B), :]), g_first))

    @pl.when(is_root)
    def _():
        left[pl.ds(0, B), B:2 * B] = jnp.zeros((B, B), F32)

    @pl.when(row == 0)
    def _():
        left[pl.ds(0, B), 0:B] = jnp.zeros((B, B), F32)

    @pl.when(row == 1)
    def _():
        left[pl.ds(0, B), 0:B] = high(pmat[1], left[pl.ds(0, B), 0:B])

    lhs = split(left[...])

    def store(r, c):
        return pltpu.make_async_copy(vals.at[r, c], out.at[r, :, c, 0, :], out_sem.at[r, c])

    @pl.loop(0, CB // 2)
    def _(j):
        c = 2 * j
        pair = lambda k: jnp.concatenate(
            [u[k, pl.ds(pl.multiple_of(c * B, B), B), :],
             u[k, pl.ds(pl.multiple_of(c * B + B, B), B), :]], axis=1)
        top = pair(0)
        top2 = split(top)
        f_row = jnp.concatenate([u[1, pl.ds(EXTRA + B + c, 1), :],
                                 u[1, pl.ds(EXTRA + B + c + 1, 1), :]], axis=1)
        low2 = split(pair(1) - f_row * dot3(q10, top2))
        rhs = tuple(jnp.concatenate([a, b], axis=0) for a, b in zip(top2, low2))
        update = dot3(lhs, rhs)
        for r in range(RB):
            for e in range(2):
                f = fill[r, 0, c + e].astype(F32)
                vals[r, c + e] = (vals[r, c + e] - update[r * B:(r + 1) * B, e * B:(e + 1) * B]) * f

        @pl.when((j == 0) & (z < 2))
        def _():
            keep = jnp.where(z == 0, panel(0), second)
            done = high(keep, jnp.where(z == 0, inverses[0], inverses[1]))
            for r in range(RB):
                if r == 0:
                    @pl.when(row > z)
                    def _():
                        vals[0, 0] = done[0:B]
                else:
                    vals[r, 0] = done[r * B:(r + 1) * B]

        for r in range(RB):
            for e in range(2):
                store(r, c + e).start()

    for d, (hops, kids) in enumerate(trees):
        for m, (bit, has) in enumerate(kids):
            @pl.when(has)
            def _():
                whole(d, m, core).wait_send()

        whole(d, 4, core).wait_send()

    for k, s, hops, get, give, dev in ways:
        for amount in (NL // 2, NL):
            @pl.when(give == amount)
            def _():
                rows = lp.at[k, pl.ds(0, amount * RL)]
                pltpu.make_async_remote_copy(
                    src_ref=rows, dst_ref=rows, send_sem=lsend.at[k, s], recv_sem=lrecv.at[k, s, 0],
                    device_id=dev).wait_send()

    for s in range(2):
        @pl.when(f_to[s])
        def _():
            fcopy(s).wait_send()

    @pl.when(is_root & (z == e_src))
    def _():
        @pl.loop(1, NZ)
        def _(j):
            extra((z + j) % NZ).wait_send()

    @pl.loop(0, CB)
    def _(c):
        for r in range(RB):
            store(r, c).wait()


def per_device(values, fill, inverses, pivots):
    shape = (RB, B, CB, 1, B)
    hbm = lambda a: pltpu.with_memory_space_constraint(a, pltpu.HBM)
    result = pl.pallas_call(
        kernel,
        out_shape=jax.ShapeDtypeStruct(shape, F32),
        in_specs=[pl.BlockSpec(memory_space=pltpu.HBM)] * 4,
        out_specs=pl.BlockSpec(memory_space=pl.ANY),
        scratch_shapes=[
            pltpu.VMEM((RB, CB, B, B), F32),
            pltpu.VMEM((2, PANEL, B), F32),
            pltpu.VMEM((2, RB * B, B), F32),
            pltpu.VMEM((2 * RB, B), F32),
            pltpu.VMEM((2, B, B), F32),
            pltpu.VMEM((2, B, B), F32),
            pltpu.VMEM((RB * B, 2 * B), F32),
            pltpu.SMEM((RB, 1, CB), jnp.int32),
            pltpu.VMEM((2, B, B), F32),
            pltpu.VMEM((2, B), jnp.int32),
            pltpu.SemaphoreType.DMA((RB, CB)),
            pltpu.SemaphoreType.DMA((RB, CB)),
            pltpu.SemaphoreType.DMA((3,)),
            pltpu.SemaphoreType.DMA((4, N + 1)),
            pltpu.SemaphoreType.DMA((4,)),
            pltpu.SemaphoreType.DMA((4, 5)),
            pltpu.SemaphoreType.DMA((2, 2, NL)),
            pltpu.SemaphoreType.DMA((2, 2)),
            pltpu.SemaphoreType.DMA(()),
            pltpu.SemaphoreType.DMA((2,)),
            pltpu.SemaphoreType.DMA((NZ,)),
            pltpu.SemaphoreType.DMA(()),
            pltpu.SemaphoreType.REGULAR((2,)),
            pltpu.SemaphoreType.REGULAR((NZ,)),
        ],
        compiler_params=pltpu.CompilerParams(
            collective_id=0, has_side_effects=True, vmem_limit_bytes=24 << 20),
    )(hbm(values.reshape(shape)), hbm(fill.reshape(RB, 1, CB)), hbm(inverses), hbm(pivots))
    return result.reshape(values.shape)


def solution(mesh):
    placed = (P(None, "row", None, None, "col", None), P(None, "row", None, "col"), P(), P())
    return jax.shard_map(
        per_device,
        mesh=mesh,
        in_specs=placed,
        out_specs=P(None, "row", None, None, "col", None),
        check_vma=False,
    )
```

```python
import jax
import jax.numpy as jnp
from jax import lax
from jax.experimental import pallas as pl
from jax.experimental.pallas import tpu as pltpu
from jax.sharding import PartitionSpec as P

HIGH = lax.Precision.HIGHEST
F32 = jnp.float32
BF16 = jnp.bfloat16
B = 128
RB = 4
CB = 16
NX = 4
NY = 4
NZ = 8
EXTRA = CB * B
ER = 40
PANEL = EXTRA + 4 * ER
N = 8
R = CB * B // 4 // N
NL = 8
RL = RB * B // NL
LA = 5
LS = 2
LB = 1
LROOT = 4


def split(x):
    hi = x.astype(BF16)
    return hi, (x - hi.astype(F32)).astype(BF16)


def dot3(a, b):
    mm = lambda u, v: jnp.dot(u, v, preferred_element_type=F32)
    return mm(a[0], b[0]) + (mm(a[0], b[1]) + mm(a[1], b[0]))


def high(a, b, dims=((1,), (0,))):
    return lax.dot_general(a, b, (dims, ((), ())), precision=HIGH, preferred_element_type=F32)


def kernel(values, fill_hbm, inverses_hbm, pivots_hbm, out, vals, u, lp, fcol, gmat, pmat, left, fill, inverses,
           pivots, load_sem, out_sem, small_sem, urecv, usib, usend, lrecv, lsend, frecv, fsend, esend, erecv,
           ready, eready):
    row = lax.axis_index("row")
    z = lax.axis_index("col")
    core = row % 2
    x = (row // 2) % NX
    y = row // (2 * NX)
    other = 1 - core
    e_src = 1 - core

    def at(x_, y_, core_, z_):
        return {"row": (y_ * NX + x_) * 2 + core_, "col": z_}

    zp, zm = (z + 1) % NZ, (z + NZ - 1) % NZ
    sibling = at(x, y, other, z)
    cube = [at(x + 1 - 2 * (x % 2), y, core, z), at(3 - x, y, core, z),
            at(x, y + 1 - 2 * (y % 2), core, z), at(x, 3 - y, core, z)]
    bits = [(x + 1) // 2 % 2, x // 2, (y + 1) // 2 % 2, y // 2]
    above, below = at(x, y, core, zp), at(x, y, core, zm)
    near = [above, below]
    is_root = row < 2

    def load(r, c):
        return pltpu.make_async_copy(values.at[r, :, c, 0, :], vals.at[r, c], load_sem.at[r, c])

    up, down = z <= 4, (z <= 1) | (z >= 5)
    from_below, from_above = (z >= 1) & (z <= 5), (z == 0) | (z >= 4)
    barrier = pltpu.get_barrier_semaphore()
    for dev in cube + [sibling]:
        pl.semaphore_signal(barrier, inc=1, device_id=dev)

    @pl.when(up)
    def _():
        pl.semaphore_signal(barrier, inc=1, device_id=above)

    @pl.when(down)
    def _():
        pl.semaphore_signal(barrier, inc=1, device_id=below)

    @pl.when(is_root & (z == e_src))
    def _():
        @pl.loop(1, NZ)
        def _(j):
            pl.semaphore_signal(barrier, inc=1, device_id=at(x, y, core, (z + j) % NZ))

    small = [pltpu.make_async_copy(fill_hbm, fill, small_sem.at[0]),
             pltpu.make_async_copy(pivots_hbm, pivots, small_sem.at[1]),
             pltpu.make_async_copy(inverses_hbm, inverses, small_sem.at[2])]
    small[0].start()

    @pl.loop(0, CB)
    def _(n):
        load(0, n % 4 * 4 + n // 4).start()

    for r in range(1, RB):
        load(r, 0).start()

    for copy in small[1:]:
        copy.start()

    @pl.loop(1, CB)
    def _(c):
        for r in range(1, RB):
            load(r, c).start()

    for copy in small:
        copy.wait()

    def inverse_products():
        for k in range(2):
            pt = (lax.broadcasted_iota(jnp.int32, (B, B), 0) == pivots[k:k + 1, :]).astype(F32)
            pmat[k] = pt
            gmat[k] = high(inverses[k], pt, ((1,), (1,)))

    pl.semaphore_wait(barrier, 5 + jnp.where(from_below, 1, 0) + jnp.where(from_above, 1, 0)
                      + jnp.where(is_root & (z != e_src), 1, 0))

    @pl.when(from_below)
    def _():
        pl.semaphore_signal(ready.at[0], inc=1, device_id=below)

    @pl.when(from_above)
    def _():
        pl.semaphore_signal(ready.at[1], inc=1, device_id=above)

    @pl.when(is_root & (z != e_src))
    def _():
        pl.semaphore_signal(eready.at[z], inc=1, device_id=at(x, y, core, e_src))

    def extra(z_):
        return pltpu.make_async_remote_copy(
            src_ref=u.at[core, pl.ds(0, B)], dst_ref=u.at[core, pl.ds(EXTRA, B)],
            send_sem=esend.at[z_], recv_sem=erecv, device_id=at(x, y, core, z_))

    @pl.when(z < 2)
    def _():
        for r in range(RB):
            f = fill[r, 0, 0].astype(F32)
            load(r, 0).wait()
            lp[z, pl.ds(r * B, B), :] = vals[r, 0] * f

            @pl.when(z == 1)
            def _():
                fcol[pl.ds(r, 1), :] = jnp.zeros((1, B), F32) + f

    @pl.when(z == 1)
    def _():
        fcol[pl.ds(RB, RB), :] = jnp.zeros((RB, B), F32)

    @pl.when(z >= 2)
    def _():
        for r in range(RB):
            load(r, 0).wait()

    @pl.when(row >= 2)
    def _():
        @pl.loop(1, CB)
        def _(c):
            load(0, c).wait()

        inverse_products()

    weight = bits[0] + bits[1] + bits[2] + bits[3]
    top = weight == 0
    trees = []
    for d in range(4):
        rel = [bits[(d + q) % 4] if q < 4 else 1 - bits[d] for q in range(1, 5)]
        last = jnp.where(rel[3] == 1, 4, jnp.where(rel[2] == 1, 3, jnp.where(rel[1] == 1, 2, rel[0])))
        hops = jnp.where(top, 0, 1 + rel[0] + rel[1] + rel[2] + rel[3])
        kids = [((d + q) % 4, last < q) for q in range(1, 4)]
        kids.append((d, top | ((last >= 1) & (last <= 3))))
        trees.append((hops, kids))

    def chunk(d, i, kind, dev):
        rows = u.at[core, pl.ds(d * 4 * B + i * R, R)]
        recv = urecv.at[d, i]
        return pltpu.make_async_remote_copy(
            src_ref=rows, dst_ref=rows, send_sem=usend.at[d, kind], recv_sem=recv, device_id=dev)

    def to_sibling(d, i):
        rows = u.at[core, pl.ds(d * 4 * B + (i - 3) * R, 4 * R)]
        return pltpu.make_async_remote_copy(
            src_ref=rows, dst_ref=rows, send_sem=usend.at[d, 4], recv_sem=usib.at[d], device_id=sibling)

    def echunk(d, kind, dev):
        rows = u.at[core, pl.ds(EXTRA + d * ER, ER)]
        recv = usib.at[d] if kind == 4 else urecv.at[d, N]
        return pltpu.make_async_remote_copy(
            src_ref=rows, dst_ref=rows, send_sem=usend.at[d, kind], recv_sem=recv, device_id=dev)

    ways = []
    for k in range(2):
        for s in range(2):
            hops = (z - k + NZ) % NZ if s == 0 else (k - z + NZ) % NZ
            count = lambda h: jnp.where(h <= 3, NL, jnp.where(h == 4, NL // 2, 0))
            ways.append((k, s, hops, count(hops), count(hops + 1), near[s]))

    def lchunk(k, s, j, dev):
        rows = lp.at[k, pl.ds((j + s * (NL // 2)) % NL * RL, RL)]
        return pltpu.make_async_remote_copy(
            src_ref=rows, dst_ref=rows, send_sem=lsend.at[k, s], recv_sem=lrecv.at[k, s, j], device_id=dev)

    def fcopy(s):
        return pltpu.make_async_remote_copy(
            src_ref=fcol, dst_ref=fcol, send_sem=fsend.at[s], recv_sem=frecv, device_id=near[s])

    f_up = (z - 1 + NZ) % NZ
    f_to = [f_up <= 3, (f_up == 0) | ((f_up >= 6))]

    early = [top | (bits[d] == 1) for d in range(4)]
    first_up, first_down = jnp.where(z >= 1, z - 1, 0), jnp.where(z == 1, 0, (NZ - z) % NZ)
    f_hops = jnp.where(f_up <= 4, f_up, NZ - f_up)

    start = jnp.where(top, LROOT, LB)

    def columns(n):
        base = n - start + LA * weight
        for s, (sends, least) in enumerate(((up, first_up), (down, first_down))):
            @pl.when(sends & (base == LA * least))
            def _():
                pl.semaphore_wait(ready.at[s], 1)

        @pl.when(base == LA * f_hops)
        def _():
            @pl.when(f_up > 0)
            def _():
                fcopy(0).wait_recv()

            for s in range(2):
                @pl.when(f_to[s])
                def _():
                    fcopy(s).start()

        for k, s, hops, get, give, dev in ways:
            due = base - LA * hops
            j = jnp.maximum(due, 0) // LS

            @pl.when((due >= 0) & (due % LS == 0) & (j < get))
            def _():
                @pl.when(hops > 0)
                def _():
                    lchunk(k, s, j, dev).wait_recv()

                @pl.when(j < give)
                def _():
                    lchunk(k, s, j, dev).start()

    def rows_of(d, i):
        @pl.when(weight > 0)
        def _():
            chunk(d, i, d, sibling).wait_recv()

        for m, (bit, has) in enumerate(trees[d][1]):
            @pl.when(has)
            def _():
                chunk(d, i, m, cube[bit]).start()

        @pl.when(i % 4 == 3)
        def _():
            to_sibling(d, i).start()

    def extra_of(d):
        @pl.when(weight > 0)
        def _():
            echunk(d, d, sibling).wait_recv()

        for m, (bit, has) in enumerate(trees[d][1]):
            @pl.when(has)
            def _():
                echunk(d, m, cube[bit]).start()

        echunk(d, 4, sibling).start()

    @pl.when(is_root)
    def _():
        for c in range(CB):
            u[core, EXTRA + B + c:EXTRA + B + c + 1, :] = jnp.zeros((1, B), F32) + fill[0, 0, c].astype(F32)

        u[core, EXTRA + B + CB:EXTRA + B + 2 * CB, :] = jnp.zeros((CB, B), F32)

    @pl.loop(jnp.minimum(start - LA * weight, 0), 0)
    def _(n):
        columns(n)

    @pl.loop(0, N)
    def _(i):
        @pl.when(is_root & (i % 2 == 0))
        def _():
            for d in range(4):
                c = 4 * d + i // 2
                if d == 0:
                    @pl.when(i > 0)
                    def _():
                        load(0, c).wait()
                else:
                    load(0, c).wait()

                u[core, pl.ds(c * B, B), :] = vals[0, c] * fill[0, 0, c].astype(F32)

        for d in range(4):
            @pl.when(early[d])
            def _():
                rows_of(d, i)

        @pl.when(is_root & (z == e_src) & (i == 0))
        def _():
            u[core, pl.ds(EXTRA, B), :] = u[core, pl.ds(0, B), :]

            pl.semaphore_wait(eready.at[1 - e_src], 1)
            extra(1 - e_src).start()

        @pl.when(is_root & (z == e_src) & (i == 3))
        def _():
            @pl.loop(2, NZ)
            def _(j):
                pl.semaphore_wait(eready.at[j], 1)
                extra(j).start()

        columns(i)

    @pl.when(is_root & (z != e_src))
    def _():
        extra(z).wait_recv()

    for d in range(4):
        @pl.when(early[d])
        def _():
            extra_of(d)

    @pl.when(is_root)
    def _():
        inverse_products()
        pmat[core] = pmat[core].T

    @pl.loop(N, jnp.maximum(LA * (4 - weight) + start + LS * NL, N))
    def _(n):
        columns(n)

        @pl.when(is_root & (n < N + CB))
        def _():
            own = pmat[core].astype(BF16)
            v = vals[0, n - N]
            first = v.astype(BF16)
            rest = v - first.astype(F32)
            second_ = rest.astype(BF16)
            third = (rest - second_.astype(F32)).astype(BF16)
            mm = lambda a: jnp.dot(own, a, preferred_element_type=F32)
            vals[0, n - N] = mm(first) + (mm(second_) + mm(third))

    panel = lambda k: lp[k]
    for half in range(2):
        if half == 1:
            g_first, g_second = split(gmat[0]), split(gmat[1])
            l_first = dot3(split(panel(0)), g_first)
            left[:, 0:B] = l_first

        for d in range(4):
            @pl.when(~early[d])
            def _():
                @pl.loop(4 * half, 4 * half + 4)
                def _(i):
                    chunk(d, i, d, sibling).wait_recv()

                to_sibling(d, 4 * half + 3).start()

    for d in range(4):
        @pl.when(~early[d])
        def _():
            echunk(d, d, sibling).wait_recv()
            echunk(d, 4, sibling).start()

    def whole(d, kind, panel):
        rows = u.at[panel, pl.ds(d * (CB * B // 4), CB * B // 4 + ER)]
        return pltpu.make_async_remote_copy(
            src_ref=rows, dst_ref=rows, send_sem=usend.at[d, kind], recv_sem=usib.at[d], device_id=sibling)

    @pl.loop(1, CB)
    def _(c):
        for r in range(1, RB):
            load(r, c).wait()

    for d in range(4):
        whole(d, 4, other).wait_recv()

    u_01 = u[0, pl.ds(EXTRA, B), :]
    f_col = jnp.concatenate(
        [jnp.broadcast_to(fcol[pl.ds(r, 1), :], (B, B)) for r in range(RB)], axis=0)
    second = panel(1) - f_col * dot3(split(l_first), split(u_01))
    left[:, B:2 * B] = dot3(split(second), g_second)
    q10 = split(dot3(split(u[1, pl.ds(EXTRA, B), :]), g_first))

    @pl.when(is_root)
    def _():
        left[pl.ds(0, B), B:2 * B] = jnp.zeros((B, B), F32)

    @pl.when(row == 0)
    def _():
        left[pl.ds(0, B), 0:B] = jnp.zeros((B, B), F32)

    @pl.when(row == 1)
    def _():
        left[pl.ds(0, B), 0:B] = high(pmat[1], left[pl.ds(0, B), 0:B])

    lhs = split(left[...])

    def store(r, c):
        return pltpu.make_async_copy(vals.at[r, c], out.at[r, :, c, 0, :], out_sem.at[r, c])

    @pl.loop(0, CB // 2, unroll=2)
    def _(j):
        c = 2 * j
        pair = lambda k: jnp.concatenate(
            [u[k, pl.ds(pl.multiple_of(c * B, B), B), :],
             u[k, pl.ds(pl.multiple_of(c * B + B, B), B), :]], axis=1)
        top = pair(0)
        top2 = split(top)
        f_row = jnp.concatenate([u[1, pl.ds(EXTRA + B + c, 1), :],
                                 u[1, pl.ds(EXTRA + B + c + 1, 1), :]], axis=1)
        low2 = split(pair(1) - f_row * dot3(q10, top2))
        rhs = tuple(jnp.concatenate([a, b], axis=0) for a, b in zip(top2, low2))
        update = dot3(lhs, rhs)
        for r in range(RB):
            for e in range(2):
                f = fill[r, 0, c + e].astype(F32)
                vals[r, c + e] = (vals[r, c + e] - update[r * B:(r + 1) * B, e * B:(e + 1) * B]) * f

        @pl.when((j == 0) & (z < 2))
        def _():
            keep = jnp.where(z == 0, panel(0), second)
            done = high(keep, jnp.where(z == 0, inverses[0], inverses[1]))
            for r in range(RB):
                if r == 0:
                    @pl.when(row > z)
                    def _():
                        vals[0, 0] = done[0:B]
                else:
                    vals[r, 0] = done[r * B:(r + 1) * B]

        for r in range(RB):
            for e in range(2):
                store(r, c + e).start()

    for d, (hops, kids) in enumerate(trees):
        for m, (bit, has) in enumerate(kids):
            @pl.when(has)
            def _():
                whole(d, m, core).wait_send()

        whole(d, 4, core).wait_send()

    for k, s, hops, get, give, dev in ways:
        for amount in (NL // 2, NL):
            @pl.when(give == amount)
            def _():
                rows = lp.at[k, pl.ds(0, amount * RL)]
                pltpu.make_async_remote_copy(
                    src_ref=rows, dst_ref=rows, send_sem=lsend.at[k, s], recv_sem=lrecv.at[k, s, 0],
                    device_id=dev).wait_send()

    for s in range(2):
        @pl.when(f_to[s])
        def _():
            fcopy(s).wait_send()

    @pl.when(is_root & (z == e_src))
    def _():
        @pl.loop(1, NZ)
        def _(j):
            extra((z + j) % NZ).wait_send()

    @pl.loop(0, CB)
    def _(c):
        for r in range(RB):
            store(r, c).wait()


def per_device(values, fill, inverses, pivots):
    shape = (RB, B, CB, 1, B)
    hbm = lambda a: pltpu.with_memory_space_constraint(a, pltpu.HBM)
    result = pl.pallas_call(
        kernel,
        out_shape=jax.ShapeDtypeStruct(shape, F32),
        in_specs=[pl.BlockSpec(memory_space=pltpu.HBM)] * 4,
        out_specs=pl.BlockSpec(memory_space=pl.ANY),
        scratch_shapes=[
            pltpu.VMEM((RB, CB, B, B), F32),
            pltpu.VMEM((2, PANEL, B), F32),
            pltpu.VMEM((2, RB * B, B), F32),
            pltpu.VMEM((2 * RB, B), F32),
            pltpu.VMEM((2, B, B), F32),
            pltpu.VMEM((2, B, B), F32),
            pltpu.VMEM((RB * B, 2 * B), F32),
            pltpu.SMEM((RB, 1, CB), jnp.int32),
            pltpu.VMEM((2, B, B), F32),
            pltpu.VMEM((2, B), jnp.int32),
            pltpu.SemaphoreType.DMA((RB, CB)),
            pltpu.SemaphoreType.DMA((RB, CB)),
            pltpu.SemaphoreType.DMA((3,)),
            pltpu.SemaphoreType.DMA((4, N + 1)),
            pltpu.SemaphoreType.DMA((4,)),
            pltpu.SemaphoreType.DMA((4, 5)),
            pltpu.SemaphoreType.DMA((2, 2, NL)),
            pltpu.SemaphoreType.DMA((2, 2)),
            pltpu.SemaphoreType.DMA(()),
            pltpu.SemaphoreType.DMA((2,)),
            pltpu.SemaphoreType.DMA((NZ,)),
            pltpu.SemaphoreType.DMA(()),
            pltpu.SemaphoreType.REGULAR((2,)),
            pltpu.SemaphoreType.REGULAR((NZ,)),
        ],
        compiler_params=pltpu.CompilerParams(
            collective_id=0, has_side_effects=True, vmem_limit_bytes=24 << 20),
    )(hbm(values.reshape(shape)), hbm(fill.reshape(RB, 1, CB)), hbm(inverses), hbm(pivots))
    return result.reshape(values.shape)


def solution(mesh):
    placed = (P(None, "row", None, None, "col", None), P(None, "row", None, "col"), P(), P())
    return jax.shard_map(
        per_device,
        mesh=mesh,
        in_specs=placed,
        out_specs=P(None, "row", None, None, "col", None),
        check_vma=False,
    )
```

```python
import jax
import jax.numpy as jnp
from jax import lax
from jax.experimental import pallas as pl
from jax.experimental.pallas import tpu as pltpu
from jax.sharding import PartitionSpec as P

HIGH = lax.Precision.HIGHEST
F32 = jnp.float32
BF16 = jnp.bfloat16
B = 128
RB = 4
CB = 16
NX = 4
NY = 4
NZ = 8
EXTRA = CB * B
ER = 40
PANEL = EXTRA + 4 * ER
N = 8
R = CB * B // 4 // N
NL = 8
RL = RB * B // NL
LA = 6
LS = 2
LB = 0
LROOT = 4


def split(x):
    hi = x.astype(BF16)
    return hi, (x - hi.astype(F32)).astype(BF16)


def dot3(a, b):
    mm = lambda u, v: jnp.dot(u, v, preferred_element_type=F32)
    return mm(a[0], b[0]) + (mm(a[0], b[1]) + mm(a[1], b[0]))


def high(a, b, dims=((1,), (0,))):
    return lax.dot_general(a, b, (dims, ((), ())), precision=HIGH, preferred_element_type=F32)


def kernel(values, fill_hbm, inverses_hbm, pivots_hbm, out, vals, u, lp, fcol, gmat, pmat, left, fill, inverses,
           pivots, load_sem, out_sem, small_sem, urecv, usib, usend, lrecv, lsend, frecv, fsend, esend, erecv,
           ready, eready):
    row = lax.axis_index("row")
    z = lax.axis_index("col")
    core = row % 2
    x = (row // 2) % NX
    y = row // (2 * NX)
    other = 1 - core
    e_src = 1 - core

    def at(x_, y_, core_, z_):
        return {"row": (y_ * NX + x_) * 2 + core_, "col": z_}

    zp, zm = (z + 1) % NZ, (z + NZ - 1) % NZ
    sibling = at(x, y, other, z)
    cube = [at(x + 1 - 2 * (x % 2), y, core, z), at(3 - x, y, core, z),
            at(x, y + 1 - 2 * (y % 2), core, z), at(x, 3 - y, core, z)]
    bits = [(x + 1) // 2 % 2, x // 2, (y + 1) // 2 % 2, y // 2]
    above, below = at(x, y, core, zp), at(x, y, core, zm)
    near = [above, below]
    is_root = row < 2

    def load(r, c):
        return pltpu.make_async_copy(values.at[r, :, c, 0, :], vals.at[r, c], load_sem.at[r, c])

    up, down = z <= 4, (z <= 1) | (z >= 5)
    from_below, from_above = (z >= 1) & (z <= 5), (z == 0) | (z >= 4)
    barrier = pltpu.get_barrier_semaphore()
    for dev in cube + [sibling]:
        pl.semaphore_signal(barrier, inc=1, device_id=dev)

    @pl.when(up)
    def _():
        pl.semaphore_signal(barrier, inc=1, device_id=above)

    @pl.when(down)
    def _():
        pl.semaphore_signal(barrier, inc=1, device_id=below)

    @pl.when(is_root & (z == e_src))
    def _():
        @pl.loop(1, NZ)
        def _(j):
            pl.semaphore_signal(barrier, inc=1, device_id=at(x, y, core, (z + j) % NZ))

    small = [pltpu.make_async_copy(fill_hbm, fill, small_sem.at[0]),
             pltpu.make_async_copy(pivots_hbm, pivots, small_sem.at[1]),
             pltpu.make_async_copy(inverses_hbm, inverses, small_sem.at[2])]
    small[0].start()

    @pl.loop(0, CB)
    def _(n):
        load(0, n % 4 * 4 + n // 4).start()

    for r in range(1, RB):
        load(r, 0).start()

    for copy in small[1:]:
        copy.start()

    @pl.loop(1, CB)
    def _(c):
        for r in range(1, RB):
            load(r, c).start()

    for copy in small:
        copy.wait()

    def inverse_products():
        for k in range(2):
            pt = (lax.broadcasted_iota(jnp.int32, (B, B), 0) == pivots[k:k + 1, :]).astype(F32)
            pmat[k] = pt
            gmat[k] = high(inverses[k], pt, ((1,), (1,)))

    pl.semaphore_wait(barrier, 5 + jnp.where(from_below, 1, 0) + jnp.where(from_above, 1, 0)
                      + jnp.where(is_root & (z != e_src), 1, 0))

    @pl.when(from_below)
    def _():
        pl.semaphore_signal(ready.at[0], inc=1, device_id=below)

    @pl.when(from_above)
    def _():
        pl.semaphore_signal(ready.at[1], inc=1, device_id=above)

    @pl.when(is_root & (z != e_src))
    def _():
        pl.semaphore_signal(eready.at[z], inc=1, device_id=at(x, y, core, e_src))

    def extra(z_):
        return pltpu.make_async_remote_copy(
            src_ref=u.at[core, pl.ds(0, B)], dst_ref=u.at[core, pl.ds(EXTRA, B)],
            send_sem=esend.at[z_], recv_sem=erecv, device_id=at(x, y, core, z_))

    @pl.when(z < 2)
    def _():
        for r in range(RB):
            f = fill[r, 0, 0].astype(F32)
            load(r, 0).wait()
            lp[z, pl.ds(r * B, B), :] = vals[r, 0] * f

            @pl.when(z == 1)
            def _():
                fcol[pl.ds(r, 1), :] = jnp.zeros((1, B), F32) + f

    @pl.when(z == 1)
    def _():
        fcol[pl.ds(RB, RB), :] = jnp.zeros((RB, B), F32)

    @pl.when(z >= 2)
    def _():
        for r in range(RB):
            load(r, 0).wait()

    @pl.when(row >= 2)
    def _():
        @pl.loop(1, CB)
        def _(c):
            load(0, c).wait()

        inverse_products()

    weight = bits[0] + bits[1] + bits[2] + bits[3]
    top = weight == 0
    trees = []
    for d in range(4):
        rel = [bits[(d + q) % 4] if q < 4 else 1 - bits[d] for q in range(1, 5)]
        last = jnp.where(rel[3] == 1, 4, jnp.where(rel[2] == 1, 3, jnp.where(rel[1] == 1, 2, rel[0])))
        hops = jnp.where(top, 0, 1 + rel[0] + rel[1] + rel[2] + rel[3])
        kids = [((d + q) % 4, last < q) for q in range(1, 4)]
        kids.append((d, top | ((last >= 1) & (last <= 3))))
        trees.append((hops, kids))

    def chunk(d, i, kind, dev):
        rows = u.at[core, pl.ds(d * 4 * B + i * R, R)]
        recv = urecv.at[d, i]
        return pltpu.make_async_remote_copy(
            src_ref=rows, dst_ref=rows, send_sem=usend.at[d, kind], recv_sem=recv, device_id=dev)

    def to_sibling(d, i):
        rows = u.at[core, pl.ds(d * 4 * B + (i - 3) * R, 4 * R)]
        return pltpu.make_async_remote_copy(
            src_ref=rows, dst_ref=rows, send_sem=usend.at[d, 4], recv_sem=usib.at[d], device_id=sibling)

    def echunk(d, kind, dev):
        rows = u.at[core, pl.ds(EXTRA + d * ER, ER)]
        recv = usib.at[d] if kind == 4 else urecv.at[d, N]
        return pltpu.make_async_remote_copy(
            src_ref=rows, dst_ref=rows, send_sem=usend.at[d, kind], recv_sem=recv, device_id=dev)

    ways = []
    for k in range(2):
        for s in range(2):
            hops = (z - k + NZ) % NZ if s == 0 else (k - z + NZ) % NZ
            count = lambda h: jnp.where(h <= 3, NL, jnp.where(h == 4, NL // 2, 0))
            ways.append((k, s, hops, count(hops), count(hops + 1), near[s]))

    def lchunk(k, s, j, dev):
        rows = lp.at[k, pl.ds((j + s * (NL // 2)) % NL * RL, RL)]
        return pltpu.make_async_remote_copy(
            src_ref=rows, dst_ref=rows, send_sem=lsend.at[k, s], recv_sem=lrecv.at[k, s, j], device_id=dev)

    def fcopy(s):
        return pltpu.make_async_remote_copy(
            src_ref=fcol, dst_ref=fcol, send_sem=fsend.at[s], recv_sem=frecv, device_id=near[s])

    f_up = (z - 1 + NZ) % NZ
    f_to = [f_up <= 3, (f_up == 0) | ((f_up >= 6))]

    early = [top | (bits[d] == 1) for d in range(4)]
    first_up, first_down = jnp.where(z >= 1, z - 1, 0), jnp.where(z == 1, 0, (NZ - z) % NZ)
    f_hops = jnp.where(f_up <= 4, f_up, NZ - f_up)

    start = jnp.where(top, LROOT, LB)

    def columns(n):
        base = n - start + LA * weight
        for s, (sends, least) in enumerate(((up, first_up), (down, first_down))):
            @pl.when(sends & (base == LA * least))
            def _():
                pl.semaphore_wait(ready.at[s], 1)

        @pl.when(base == LA * f_hops)
        def _():
            @pl.when(f_up > 0)
            def _():
                fcopy(0).wait_recv()

            for s in range(2):
                @pl.when(f_to[s])
                def _():
                    fcopy(s).start()

        for k, s, hops, get, give, dev in ways:
            due = base - LA * hops
            j = jnp.maximum(due, 0) // LS

            @pl.when((due >= 0) & (due % LS == 0) & (j < get))
            def _():
                @pl.when(hops > 0)
                def _():
                    lchunk(k, s, j, dev).wait_recv()

                @pl.when(j < give)
                def _():
                    lchunk(k, s, j, dev).start()

    def rows_of(d, i):
        @pl.when(weight > 0)
        def _():
            chunk(d, i, d, sibling).wait_recv()

        for m, (bit, has) in enumerate(trees[d][1]):
            @pl.when(has)
            def _():
                chunk(d, i, m, cube[bit]).start()

        @pl.when(i % 4 == 3)
        def _():
            to_sibling(d, i).start()

    def extra_of(d):
        @pl.when(weight > 0)
        def _():
            echunk(d, d, sibling).wait_recv()

        for m, (bit, has) in enumerate(trees[d][1]):
            @pl.when(has)
            def _():
                echunk(d, m, cube[bit]).start()

        echunk(d, 4, sibling).start()

    @pl.when(is_root)
    def _():
        for c in range(CB):
            u[core, EXTRA + B + c:EXTRA + B + c + 1, :] = jnp.zeros((1, B), F32) + fill[0, 0, c].astype(F32)

        u[core, EXTRA + B + CB:EXTRA + B + 2 * CB, :] = jnp.zeros((CB, B), F32)

    @pl.loop(jnp.minimum(start - LA * weight, 0), 0)
    def _(n):
        columns(n)

    @pl.loop(0, N)
    def _(i):
        @pl.when(is_root & (i % 2 == 0))
        def _():
            for d in range(4):
                c = 4 * d + i // 2
                if d == 0:
                    @pl.when(i > 0)
                    def _():
                        load(0, c).wait()
                else:
                    load(0, c).wait()

                u[core, pl.ds(c * B, B), :] = vals[0, c] * fill[0, 0, c].astype(F32)

        for d in range(4):
            @pl.when(early[d])
            def _():
                rows_of(d, i)

        @pl.when(is_root & (z == e_src) & (i == 0))
        def _():
            u[core, pl.ds(EXTRA, B), :] = u[core, pl.ds(0, B), :]

            pl.semaphore_wait(eready.at[1 - e_src], 1)
            extra(1 - e_src).start()

        @pl.when(is_root & (z == e_src) & (i == 3))
        def _():
            @pl.loop(2, NZ)
            def _(j):
                pl.semaphore_wait(eready.at[j], 1)
                extra(j).start()

        columns(i)

    @pl.when(is_root & (z != e_src))
    def _():
        extra(z).wait_recv()

    for d in range(4):
        @pl.when(early[d])
        def _():
            extra_of(d)

    @pl.when(is_root)
    def _():
        inverse_products()
        pmat[core] = pmat[core].T

    @pl.loop(N, jnp.maximum(LA * (4 - weight) + start + LS * NL, N))
    def _(n):
        columns(n)

        @pl.when(is_root & (n < N + CB))
        def _():
            own = pmat[core].astype(BF16)
            v = vals[0, n - N]
            first = v.astype(BF16)
            rest = v - first.astype(F32)
            second_ = rest.astype(BF16)
            third = (rest - second_.astype(F32)).astype(BF16)
            mm = lambda a: jnp.dot(own, a, preferred_element_type=F32)
            vals[0, n - N] = mm(first) + (mm(second_) + mm(third))

    panel = lambda k: lp[k]
    for half in range(2):
        if half == 1:
            g_first, g_second = split(gmat[0]), split(gmat[1])
            l_first = dot3(split(panel(0)), g_first)
            left[:, 0:B] = l_first

        for d in range(4):
            @pl.when(~early[d])
            def _():
                @pl.loop(4 * half, 4 * half + 4)
                def _(i):
                    chunk(d, i, d, sibling).wait_recv()

                to_sibling(d, 4 * half + 3).start()

    for d in range(4):
        @pl.when(~early[d])
        def _():
            echunk(d, d, sibling).wait_recv()
            echunk(d, 4, sibling).start()

    def whole(d, kind, panel):
        rows = u.at[panel, pl.ds(d * (CB * B // 4), CB * B // 4 + ER)]
        return pltpu.make_async_remote_copy(
            src_ref=rows, dst_ref=rows, send_sem=usend.at[d, kind], recv_sem=usib.at[d], device_id=sibling)

    @pl.loop(1, CB)
    def _(c):
        for r in range(1, RB):
            load(r, c).wait()

    for d in range(4):
        whole(d, 4, other).wait_recv()

    u_01 = u[0, pl.ds(EXTRA, B), :]
    f_col = jnp.concatenate(
        [jnp.broadcast_to(fcol[pl.ds(r, 1), :], (B, B)) for r in range(RB)], axis=0)
    second = panel(1) - f_col * dot3(split(l_first), split(u_01))
    left[:, B:2 * B] = dot3(split(second), g_second)
    q10 = split(dot3(split(u[1, pl.ds(EXTRA, B), :]), g_first))

    @pl.when(is_root)
    def _():
        left[pl.ds(0, B), B:2 * B] = jnp.zeros((B, B), F32)

    @pl.when(row == 0)
    def _():
        left[pl.ds(0, B), 0:B] = jnp.zeros((B, B), F32)

    @pl.when(row == 1)
    def _():
        left[pl.ds(0, B), 0:B] = high(pmat[1], left[pl.ds(0, B), 0:B])

    lhs = split(left[...])

    def store(r, c):
        return pltpu.make_async_copy(vals.at[r, c], out.at[r, :, c, 0, :], out_sem.at[r, c])

    @pl.loop(0, CB // 2, unroll=2)
    def _(j):
        c = 2 * j
        pair = lambda k: jnp.concatenate(
            [u[k, pl.ds(pl.multiple_of(c * B, B), B), :],
             u[k, pl.ds(pl.multiple_of(c * B + B, B), B), :]], axis=1)
        top = pair(0)
        top2 = split(top)
        f_row = jnp.concatenate([u[1, pl.ds(EXTRA + B + c, 1), :],
                                 u[1, pl.ds(EXTRA + B + c + 1, 1), :]], axis=1)
        low2 = split(pair(1) - f_row * dot3(q10, top2))
        rhs = tuple(jnp.concatenate([a, b], axis=0) for a, b in zip(top2, low2))
        update = dot3(lhs, rhs)
        for r in range(RB):
            for e in range(2):
                f = fill[r, 0, c + e].astype(F32)
                vals[r, c + e] = (vals[r, c + e] - update[r * B:(r + 1) * B, e * B:(e + 1) * B]) * f

        @pl.when((j == 0) & (z < 2))
        def _():
            keep = jnp.where(z == 0, panel(0), second)
            done = high(keep, jnp.where(z == 0, inverses[0], inverses[1]))
            for r in range(RB):
                if r == 0:
                    @pl.when(row > z)
                    def _():
                        vals[0, 0] = done[0:B]
                else:
                    vals[r, 0] = done[r * B:(r + 1) * B]

        for r in range(RB):
            for e in range(2):
                store(r, c + e).start()

    for d, (hops, kids) in enumerate(trees):
        for m, (bit, has) in enumerate(kids):
            @pl.when(has)
            def _():
                whole(d, m, core).wait_send()

        whole(d, 4, core).wait_send()

    for k, s, hops, get, give, dev in ways:
        for amount in (NL // 2, NL):
            @pl.when(give == amount)
            def _():
                rows = lp.at[k, pl.ds(0, amount * RL)]
                pltpu.make_async_remote_copy(
                    src_ref=rows, dst_ref=rows, send_sem=lsend.at[k, s], recv_sem=lrecv.at[k, s, 0],
                    device_id=dev).wait_send()

    for s in range(2):
        @pl.when(f_to[s])
        def _():
            fcopy(s).wait_send()

    @pl.when(is_root & (z == e_src))
    def _():
        @pl.loop(1, NZ)
        def _(j):
            extra((z + j) % NZ).wait_send()

    @pl.loop(0, CB)
    def _(c):
        for r in range(RB):
            store(r, c).wait()


def per_device(values, fill, inverses, pivots):
    shape = (RB, B, CB, 1, B)
    hbm = lambda a: pltpu.with_memory_space_constraint(a, pltpu.HBM)
    result = pl.pallas_call(
        kernel,
        out_shape=jax.ShapeDtypeStruct(shape, F32),
        in_specs=[pl.BlockSpec(memory_space=pltpu.HBM)] * 4,
        out_specs=pl.BlockSpec(memory_space=pl.ANY),
        scratch_shapes=[
            pltpu.VMEM((RB, CB, B, B), F32),
            pltpu.VMEM((2, PANEL, B), F32),
            pltpu.VMEM((2, RB * B, B), F32),
            pltpu.VMEM((2 * RB, B), F32),
            pltpu.VMEM((2, B, B), F32),
            pltpu.VMEM((2, B, B), F32),
            pltpu.VMEM((RB * B, 2 * B), F32),
            pltpu.SMEM((RB, 1, CB), jnp.int32),
            pltpu.VMEM((2, B, B), F32),
            pltpu.VMEM((2, B), jnp.int32),
            pltpu.SemaphoreType.DMA((RB, CB)),
            pltpu.SemaphoreType.DMA((RB, CB)),
            pltpu.SemaphoreType.DMA((3,)),
            pltpu.SemaphoreType.DMA((4, N + 1)),
            pltpu.SemaphoreType.DMA((4,)),
            pltpu.SemaphoreType.DMA((4, 5)),
            pltpu.SemaphoreType.DMA((2, 2, NL)),
            pltpu.SemaphoreType.DMA((2, 2)),
            pltpu.SemaphoreType.DMA(()),
            pltpu.SemaphoreType.DMA((2,)),
            pltpu.SemaphoreType.DMA((NZ,)),
            pltpu.SemaphoreType.DMA(()),
            pltpu.SemaphoreType.REGULAR((2,)),
            pltpu.SemaphoreType.REGULAR((NZ,)),
        ],
        compiler_params=pltpu.CompilerParams(
            collective_id=0, has_side_effects=True, vmem_limit_bytes=24 << 20),
    )(hbm(values.reshape(shape)), hbm(fill.reshape(RB, 1, CB)), hbm(inverses), hbm(pivots))
    return result.reshape(values.shape)


def solution(mesh):
    placed = (P(None, "row", None, None, "col", None), P(None, "row", None, "col"), P(), P())
    return jax.shard_map(
        per_device,
        mesh=mesh,
        in_specs=placed,
        out_specs=P(None, "row", None, None, "col", None),
        check_vma=False,
    )
```
